32 devices in a mesh: seq: 16 (over z, y, x), head: 2 (over core).
Axes of the slice: x: 2, y: 2, z: 4, core: 2. Of those that a mesh axis runs over, the one named last changes fastest.
Arguments:
- x_in: bfloat16 [2816, 1024], P('seq'), may hold values from -7 to 7
- seg_ids: int32 [2816], replicated, may hold values from 0 to 6, never falling along the last dimension, each value on 1 to 2112 neighbouring positions
- decay_exp: int32 [24], P('head'), may hold values from 3 to 16
- cotangent: bfloat16 [2816, 1024], P('seq'), may hold values from -6 to 6
- w_zx: bfloat16 [1024, 2, 1536], P('seq', None, 'head'), may hold values from -0.1875 to 0.1875
- w_bc: bfloat16 [1024, 256], P('seq'), may hold values from -0.1875 to 0.1875
- w_dt: bfloat16 [1024, 24], P('seq', 'head'), may hold values from -0.1875 to 0.1875
- w_mout: bfloat16 [1536, 1024], P('head', 'seq'), may hold values from -0.15625 to 0.15625
- w_q: bfloat16 [1024, 512], P('seq', 'head'), may hold values from -0.1875 to 0.1875
- w_kv: bfloat16 [1024, 2, 128], P('seq', None, 'head'), may hold values from -0.1875 to 0.1875
- w_ao: bfloat16 [512, 1024], P('head', 'seq'), may hold values from -3.5 to 3.5
- w_gu: bfloat16 [1024, 2, 2048], P('seq', None, 'head'), may hold values from -0.1875 to 0.1875
- w_down: bfloat16 [2048, 1024], P('head', 'seq'), may hold values from -0.125 to 0.125
- norm1_gain: float32 [1024], replicated, may hold values from 0.25 to 1.75
- norm2_gain: float32 [1024], replicated, may hold values from 0.25 to 1.75
- mnorm_gain: float32 [1536], P('head'), may hold values from 0.25 to 1.75
- conv_x: float32 [4, 1536], P(None, 'head'), may hold values from -3 to 3
- conv_bc: float32 [4, 256], replicated, may hold values from -3 to 3
- dt_bias: float32 [24], P('head'), may hold values from -2 to 1
- skip_d: float32 [24], P('head'), may hold values from 0.5 to 1.5
Outputs:
- output: bfloat16 [2816, 1024], P('seq')
- x_grad: float32 [2816, 1024], P('seq')
- w_zx_grad: float32 [1024, 2, 1536], P('seq', None, 'head')
- w_bc_grad: float32 [1024, 256], P('seq')
- w_dt_grad: float32 [1024, 24], P('seq', 'head')
- w_mout_grad: float32 [1536, 1024], P('head', 'seq')
- w_q_grad: float32 [1024, 512], P('seq', 'head')
- w_kv_grad: float32 [1024, 2, 128], P('seq', None, 'head')
- w_ao_grad: float32 [512, 1024], P('head', 'seq')
- w_gu_grad: float32 [1024, 2, 2048], P('seq', None, 'head')
- w_down_grad: float32 [2048, 1024], P('head', 'seq')
- norm1_gain_grad: float32 [1024], replicated
- norm2_gain_grad: float32 [1024], replicated
- mnorm_gain_grad: float32 [1536], P('head')
- conv_x_grad: float32 [4, 1536], P(None, 'head')
- conv_bc_grad: float32 [4, 256], replicated
- dt_bias_grad: float32 [24], P('head')
- skip_d_grad: float32 [24], P('head')
The draws below stay inside these ranges and needn't reach their ends.
Inputs may be any that keep to these rules, and one draw needn't show every extreme that they name: `seg_ids`: sequence ids never fall along the tokens; every id is used, each sequence holds at most 2112 consecutive tokens, and some sequence holds exactly 2112.
All inputs are finite; a program needn't handle non-finite values.
Results may differ from the reference program's by a relative error of at most 0.01225.
The reference program's roundings to bfloat16 on the way count: a program that leaves them out, or rounds other values in their place, can miss the bound.
Values may be sent and summed in bfloat16 or wider, within the bound.
A program may use at most 256 MiB of HBM per device.

```python
import math
import jax
import jax.numpy as jnp
import numpy as np
from jax import lax

D = 1024
MI = 1536
MH = 24
MP = 64
NS = 128
KC = 4
AH = 8
KVH = 2
AD = 64
FF = 2048
TOK_DEV = 176
EXP_TOP = 16
SEQS = 7
SEQ_MAX = 2112
TOKENS = 2816
N_HEAD = 2


def draw_x_in(key, part):
    noise_key = jax.random.fold_in(key, 7011)
    values = jax.random.truncated_normal(noise_key, -6.0, 6.0, (TOKENS, D), jnp.float32)
    return values.astype(jnp.bfloat16)


def draw_w_q(key, part):
    weight_key = jax.random.fold_in(key, 7021)
    column_count = AH * AD
    values = jax.random.truncated_normal(weight_key, -6.0, 6.0, (D, column_count), jnp.float32) / D ** 0.5
    return values.astype(jnp.bfloat16)


def draw_w_kv(key, part):
    weight_key = jax.random.fold_in(key, 7031)
    column_count = KVH * AD
    values = jax.random.truncated_normal(weight_key, -6.0, 6.0, (D, 2, column_count), jnp.float32) / D ** 0.5
    return values.astype(jnp.bfloat16)


def place_ends(drawn, stream_key, low, top_value):
    shape = drawn.shape
    index_at = [jax.random.randint(jax.random.fold_in(stream_key, axis), (), 0, shape[axis]) for axis in range(len(shape))]
    drawn = drawn.at[tuple(index_at)].set(low)
    longest = shape.index(max(shape))
    index_at[longest] = (index_at[longest] + 1) % shape[longest]
    return drawn.at[tuple(index_at)].set(top_value)


def shard_levels(rng, extent, split, low, high):
    level = 1.0
    for dim, shards_of in split:
        heights = jax.random.uniform(jax.random.fold_in(jax.random.fold_in(rng, 6), dim), (shards_of,), jnp.float32, low / len(split), high / len(split))
        level = level * jnp.repeat(jnp.exp(heights), extent[dim] // shards_of).reshape((-1,) + (1,) * (len(extent) - 1 - dim))
    return level


def length_profile(amount, total, reach, skew):
    weights = [(1 << 20) // math.isqrt(standing ** skew) + 1 for standing in range(2, amount + 1)]
    surplus, holding = total - reach - (amount - 1), [1] * (amount - 1)
    while surplus > 0:
        movable = [i for i in range(amount - 1) if holding[i] < reach]
        mass, left = sum([weights[i] for i in movable]), surplus
        for i in movable:
            addition = min(reach - holding[i], max(1, left * weights[i] // mass), surplus)
            holding[i] = holding[i] + addition
            surplus = surplus - addition
    return np.array([reach] + holding)


def uneven(own_key, number_of, total, bound, lean):
    if number_of == 2:
        one = jax.random.randint(own_key, (), max(1, total - bound), min(bound, total - 1) + 1)
        return jnp.stack([one, total - one])
    sizes = jnp.asarray(length_profile(number_of, total, bound, lean), jnp.int32)
    couples = (number_of - 1) // 2
    donor, receiver = sizes[1:1 + 2 * couples:2], sizes[2:2 + 2 * couples:2]
    room = jnp.minimum(donor - 1, bound - receiver)
    shifted = jax.random.randint(jax.random.fold_in(own_key, 1), (couples,), 0, 1 << 20) % (room + 1)
    sizes = sizes.at[1:1 + 2 * couples:2].set(donor - shifted).at[2:2 + 2 * couples:2].set(receiver + shifted)
    return sizes[jax.random.permutation(jax.random.fold_in(own_key, 2), number_of)]


def bell_draw(own_key, extent, scale, reach, shards=(), held_as=jnp.bfloat16):
    array = jax.random.normal(own_key, extent, jnp.float32) * scale
    if len(shards) > 0:
        array = shard_levels(own_key, extent, shards, -0.22, 0.18) * array
    return jnp.clip(array, min=-reach, max=reach).astype(held_as)


def setup_inputs(seed: int = 0) -> dict:
    streams_of = jax.random.split(jax.random.key(seed), 21)
    return {
        "x_in": draw_x_in(jax.random.fold_in(streams_of[20], 71), 0),
        "seg_ids": jnp.searchsorted(jnp.cumsum(uneven(streams_of[1], SEQS, TOKENS, SEQ_MAX, 0)), jnp.arange(TOKENS), side="right").astype(jnp.int32),
        "decay_exp": place_ends(jax.random.randint(streams_of[2], (MH,), 3, EXP_TOP + 1), jax.random.fold_in(streams_of[2], 1), 3, EXP_TOP).astype(jnp.int32),
        "cotangent": bell_draw(streams_of[3], (TOKENS, D), 1.0, 6.0, ((0, 16),)),
        "w_zx": bell_draw(streams_of[4], (D, 2, MI), D ** -0.5, 0.1875, ((0, 16), (2, 2))),
        "w_bc": bell_draw(streams_of[5], (D, 2 * NS), D ** -0.5, 0.1875, ((0, 16),)),
        "w_dt": bell_draw(streams_of[6], (D, MH), D ** -0.5, 0.1875, ((0, 16), (1, 2))),
        "w_mout": bell_draw(streams_of[7], (MI, D), MI ** -0.5, 0.15625, ((0, 2), (1, 16))),
        "w_q": draw_w_q(jax.random.fold_in(streams_of[20], 71), 0),
        "w_kv": draw_w_kv(jax.random.fold_in(streams_of[20], 71), 0),
        "w_ao": bell_draw(streams_of[10], (AH * AD, D), (max(1, AH * AD * 16 // SEQ_MAX)) ** -0.5, 3.5, ((0, 2), (1, 16))),
        "w_gu": bell_draw(streams_of[11], (D, 2, FF), D ** -0.5, 0.1875, ((0, 16), (2, 2))),
        "w_down": bell_draw(streams_of[12], (FF, D), FF ** -0.5, 0.125, ((0, 2), (1, 16))),
        "norm1_gain": jnp.clip(1.0 + 0.15 * jax.random.normal(streams_of[13], (D,), jnp.float32), 0.25, 1.75),
        "norm2_gain": jnp.clip(1.0 + 0.15 * jax.random.normal(streams_of[14], (D,), jnp.float32), 0.25, 1.75),
        "mnorm_gain": jnp.clip(1.0 + 0.15 * jax.random.normal(streams_of[15], (MI,), jnp.float32), 0.25, 1.75),
        "conv_x": bell_draw(streams_of[16], (KC, MI), 0.5, 3.0, ((1, 2),), jnp.float32),
        "conv_bc": bell_draw(streams_of[17], (KC, 2 * NS), 0.5, 3.0, (), jnp.float32),
        "dt_bias": jnp.clip(-2.0 + 3.0 * jax.random.uniform(streams_of[18], (MH,), jnp.float32) ** shard_levels(streams_of[18], (MH,), ((0, 2),), -0.2, 0.2), -2.0, 1.0),
        "skip_d": jnp.clip(0.5 + 1.0 * jax.random.uniform(streams_of[19], (MH,), jnp.float32) ** shard_levels(streams_of[19], (MH,), ((0, 2),), -0.2, 0.2), 0.5, 1.5),
    }


epsilon = 1e-05
key_multiplier = 0.390625
attention_multiplier = 0.9375
mamba_multiplier = 0.5
gate_multiplier = 0.75
down_multiplier = 0.5
rope_base = 100000000000.0
far_below = -1e+30
highest = lax.Precision.HIGHEST

def silu_grad(values):
    sigmoid_value = jax.nn.sigmoid(values)
    return sigmoid_value * (1.0 + values * (1.0 - sigmoid_value))

def rotate(values, positions, direction):
    half_dim = values.shape[-1] // 2
    frequency = jnp.power(jnp.float32(rope_base), -jnp.arange(half_dim, dtype=jnp.float32) / half_dim)
    angles = positions.astype(jnp.float32)[:, None] * frequency[None, :]
    cosine = jnp.cos(angles)[:, None, :]
    sine_part = direction * jnp.sin(angles)[:, None, :]
    first_half = values[..., :half_dim]
    second_half = values[..., half_dim:]
    return jnp.concatenate([first_half * cosine - second_half * sine_part, second_half * cosine + first_half * sine_part], axis=-1)

def conv_masks(conv_seg, tap_count):
    row_count = conv_seg.shape[0] - tap_count + 1
    own_seg = conv_seg[tap_count - 1:]
    return [conv_seg[tap_index:tap_index + row_count] == own_seg for tap_index in range(tap_count)]

def conv_apply(extended, keep_list, weight):
    row_count = keep_list[0].shape[0]
    result = jnp.zeros((row_count, extended.shape[1]), jnp.float32)
    for tap_index in range(weight.shape[0]):
        result = result + weight[tap_index][None, :] * jnp.where(keep_list[tap_index][:, None], extended[tap_index:tap_index + row_count], 0.0)
    return result

def conv_grads(extended, keep_list, weight, grad_pre):
    row_count = grad_pre.shape[0]
    grad_ext = jnp.zeros(extended.shape, jnp.float32)
    weight_parts = []
    for tap_index in range(weight.shape[0]):
        masked = jnp.where(keep_list[tap_index][:, None], grad_pre, 0.0)
        grad_ext = grad_ext.at[tap_index:tap_index + row_count].add(weight[tap_index][None, :] * masked)
        weight_parts.append(lax.optimization_barrier(jnp.sum(masked * extended[tap_index:tap_index + row_count], axis=0)))
    return (grad_ext, jnp.stack(weight_parts))

def lower_ones(row_count):
    row_ids = jnp.arange(row_count, dtype=jnp.int32)
    return (row_ids[:, None] >= row_ids[None, :]).astype(jnp.float32)

def ssd_out(channels, b_matrix, c_matrix, log_decay, step_size, state_in, skip_gain, pair_keep, first_keep):
    row_count, head_count = log_decay.shape
    cumulative = jnp.dot(lower_ones(row_count), log_decay, precision=highest)
    cum_heads = cumulative.T
    difference = cum_heads[:, :, None] - cum_heads[:, None, :]
    decay_matrix = jnp.where(pair_keep[None], jnp.exp(jnp.where(pair_keep[None], difference, 0.0)), 0.0)
    inner_product = jnp.dot(c_matrix, b_matrix.T, precision=highest)
    mixing = decay_matrix * inner_product[None]
    inputs = channels.reshape(row_count, head_count, -1)
    scaled = inputs * step_size[:, :, None]
    result = jnp.einsum('hts,shp->thp', mixing, scaled, precision=highest)
    carried = jnp.einsum('tn,hpn->thp', c_matrix, state_in, precision=highest)
    result = result + (jnp.exp(cumulative) * first_keep[:, None])[:, :, None] * carried + skip_gain[None, :, None] * inputs
    return result.reshape(row_count, -1)

def ssd_end(channels, b_matrix, log_decay, step_size, state_in, first_keep, last_keep):
    row_count, head_count = log_decay.shape
    cumulative = jnp.dot(lower_ones(row_count), log_decay, precision=highest)
    whole_sum = cumulative[-1]
    tail_decay = jnp.exp(whole_sum[None, :] - cumulative) * last_keep[:, None]
    scaled = channels.reshape(row_count, head_count, -1) * (step_size * tail_decay)[:, :, None]
    end_state = jnp.einsum('thp,tn->hpn', scaled, b_matrix, precision=highest)
    carry_factor = jnp.exp(whole_sum) * first_keep[-1]
    return (end_state + carry_factor[:, None, None] * state_in, carry_factor)

def attend(query_rows, window_kv, keep_mask):
    key_rows = window_kv[:, :AD].astype(jnp.float32)
    value_rows = window_kv[:, AD:].astype(jnp.float32)
    scores = jnp.einsum('tgd,kd->gtk', query_rows.astype(jnp.float32), key_rows) * AD ** (-0.5)
    masked = jnp.where(keep_mask[None], scores, far_below)
    row_top = lax.optimization_barrier(jnp.max(masked, axis=-1, keepdims=True))
    weights = jnp.exp(masked - row_top)
    weight_total = lax.optimization_barrier(jnp.sum(weights, axis=-1, keepdims=True))
    log_sum = row_top + jnp.log(weight_total)
    probabilities = (weights / weight_total).astype(jnp.bfloat16)
    result = jnp.einsum('gtk,kd->tgd', probabilities.astype(jnp.float32), value_rows)
    return (result.astype(jnp.bfloat16), log_sum)

def attend_back(query_rows, window_kv, keep_mask, log_sum, out_rows, grad_rows):
    key_rows = window_kv[:, :AD].astype(jnp.float32)
    value_rows = window_kv[:, AD:].astype(jnp.float32)
    query_float = query_rows.astype(jnp.float32)
    grad_float = grad_rows.astype(jnp.float32)
    scores = jnp.einsum('tgd,kd->gtk', query_float, key_rows) * AD ** (-0.5)
    probabilities = jnp.exp(jnp.where(keep_mask[None], scores - log_sum, far_below))
    row_delta = lax.optimization_barrier(jnp.sum(grad_float * out_rows.astype(jnp.float32), axis=-1)).T
    grad_probs = jnp.einsum('tgd,kd->gtk', grad_float, value_rows)
    grad_scores = (probabilities * (grad_probs - row_delta[:, :, None])).astype(jnp.bfloat16).astype(jnp.float32)
    probs_rounded = probabilities.astype(jnp.bfloat16).astype(jnp.float32)
    grad_query = jnp.einsum('gtk,kd->tgd', grad_scores, key_rows) * AD ** (-0.5)
    grad_keys = jnp.einsum('gtk,tgd->kd', grad_scores, query_float) * AD ** (-0.5)
    grad_values = jnp.einsum('gtk,tgd->kd', probs_rounded, grad_float)
    return (grad_query, jnp.concatenate([grad_keys, grad_values], axis=-1))

def product_t(left, right):
    return jnp.einsum('tc,td->cd', left.astype(jnp.float32), right.astype(jnp.float32))

def reference(x_in, seg_ids, decay_exp, cotangent, w_zx, w_bc, w_dt, w_mout, w_q, w_kv, w_ao, w_gu, w_down, norm1_gain, norm2_gain, mnorm_gain, conv_x, conv_bc, dt_bias, skip_d):
    tok_rows = TOK_DEV
    block_count = TOKENS // TOK_DEV
    window_blocks = SEQ_MAX // TOK_DEV + 1
    group_count = N_HEAD
    tap_count = KC
    inner_half = MI // group_count
    heads_here = MH // group_count
    q_heads = AH // group_count
    pad_rows = window_blocks * tok_rows
    positions = jnp.arange(TOKENS, dtype=jnp.int32)
    token_ids = jnp.arange(tok_rows, dtype=jnp.int32)
    seg_front = jnp.concatenate([jnp.full((pad_rows,), -1, jnp.int32), seg_ids.astype(jnp.int32)])
    conv_keeps = conv_masks(seg_front[pad_rows - tap_count + 1:], tap_count)
    seg_blocks = seg_ids.astype(jnp.int32).reshape(block_count, tok_rows)
    prev_blocks = seg_front[pad_rows - 1:pad_rows - 1 + TOKENS].reshape(block_count, tok_rows)[:, 0]
    pair_keep = (token_ids[:, None] >= token_ids[None, :])[None] & (seg_blocks[:, :, None] == seg_blocks[:, None, :])
    first_keep = (seg_blocks == prev_blocks[:, None]).astype(jnp.float32)
    last_keep = (seg_blocks == seg_blocks[:, -1:]).astype(jnp.float32)

    def attention_keep(start_row):
        query_pos = start_row + token_ids
        key_pos = start_row - (window_blocks - 1) * tok_rows + jnp.arange(window_blocks * tok_rows, dtype=jnp.int32)
        own_seg = lax.dynamic_slice_in_dim(seg_front, start_row + pad_rows, tok_rows)
        key_seg = lax.dynamic_slice_in_dim(seg_front, start_row + tok_rows, window_blocks * tok_rows)
        return (key_pos[None, :] <= query_pos[:, None]) & (key_seg[None, :] == own_seg[:, None])
    x_float = x_in.astype(jnp.float32)
    norm_one = lax.rsqrt(lax.optimization_barrier(jnp.mean(x_float * x_float, axis=-1, keepdims=True)) + epsilon)
    normed = (x_float * norm_one * norm1_gain).astype(jnp.bfloat16)
    bc_send = jnp.dot(normed, w_bc, preferred_element_type=jnp.float32).astype(jnp.bfloat16)
    ext_bc = jnp.concatenate([jnp.zeros((tap_count - 1, 2 * NS), jnp.float32), bc_send.astype(jnp.float32)], 0)
    pre_bc = conv_apply(ext_bc, conv_keeps, conv_bc)
    conv_bcs = jax.nn.silu(pre_bc)
    b_matrix = conv_bcs[:, :NS]
    c_matrix = conv_bcs[:, NS:]
    rate_all = -jnp.exp2(-decay_exp.astype(jnp.float32)) * (256.0 / TOK_DEV)
    mamba_total = jnp.zeros((TOKENS, D), jnp.float32)
    attn_total = jnp.zeros((TOKENS, D), jnp.float32)
    square_total = jnp.zeros((TOKENS,), jnp.float32)
    saved = []
    for group_index in range(group_count):
        chan_low = group_index * inner_half
        head_low = group_index * heads_here
        attn_low = group_index * q_heads * AD
        zx_weight = w_zx[:, :, chan_low:chan_low + inner_half].reshape(D, 2 * inner_half)
        dt_weight = w_dt[:, head_low:head_low + heads_here]
        zx_proj = jnp.dot(normed, zx_weight, preferred_element_type=jnp.float32)
        gate_z = zx_proj[:, :inner_half]
        x_send = zx_proj[:, inner_half:].astype(jnp.bfloat16)
        dt_raw = jnp.dot(normed, dt_weight, preferred_element_type=jnp.float32) + dt_bias[head_low:head_low + heads_here]
        ext_x = jnp.concatenate([jnp.zeros((tap_count - 1, inner_half), jnp.float32), x_send.astype(jnp.float32)], 0)
        conv_weight_x = conv_x[:, chan_low:chan_low + inner_half]
        pre_x = conv_apply(ext_x, conv_keeps, conv_weight_x)
        conv_xs = jax.nn.silu(pre_x)
        step_size = jax.nn.softplus(dt_raw)
        rate = rate_all[head_low:head_low + heads_here]
        log_decay = step_size * rate[None, :]
        skip_gain = skip_d[head_low:head_low + heads_here]
        zero_state = jnp.zeros((heads_here, MP, NS), jnp.float32)
        pieces = (conv_xs.reshape(block_count, tok_rows, inner_half), b_matrix.reshape(block_count, tok_rows, NS), c_matrix.reshape(block_count, tok_rows, NS), log_decay.reshape(block_count, tok_rows, heads_here), step_size.reshape(block_count, tok_rows, heads_here), pair_keep, first_keep, last_keep)

        def forward_block(state_in, block_pieces, skip_gain=skip_gain):
            block_xs, block_b, block_c, block_log, block_step, block_pair, block_first, block_last = block_pieces
            block_y = ssd_out(block_xs, block_b, block_c, block_log, block_step, state_in, skip_gain, block_pair, block_first)
            end_state, _ = ssd_end(block_xs, block_b, block_log, block_step, state_in, block_first, block_last)
            return (end_state, (block_y, state_in))
        _, (ssd_blocks, states_in) = lax.scan(forward_block, zero_state, pieces)
        ssd_y = ssd_blocks.reshape(TOKENS, inner_half)
        silu_z = jax.nn.silu(gate_z)
        gated = ssd_y * silu_z
        square_total = square_total + lax.optimization_barrier(jnp.sum(gated * gated, axis=-1))
        gain_part = mnorm_gain[chan_low:chan_low + inner_half]
        mamba_in = (gated * gain_part).astype(jnp.bfloat16)
        mout_weight = w_mout[chan_low:chan_low + inner_half]
        mamba_total = mamba_total + jnp.dot(mamba_in, mout_weight, preferred_element_type=jnp.float32)
        q_weight = w_q[:, attn_low:attn_low + q_heads * AD]
        kv_weight = w_kv[:, :, group_index * AD:(group_index + 1) * AD].reshape(D, 2 * AD)
        query_raw = jnp.dot(normed, q_weight, preferred_element_type=jnp.float32).reshape(TOKENS, q_heads, AD)
        keyval = jnp.dot(normed, kv_weight, preferred_element_type=jnp.float32)
        query16 = rotate(query_raw, positions, 1.0).astype(jnp.bfloat16)
        key_rot = rotate(keyval[:, None, :AD] * key_multiplier, positions, 1.0)[:, 0, :]
        kv_send = jnp.concatenate([key_rot, keyval[:, AD:]], axis=-1).astype(jnp.bfloat16)
        kv_front = jnp.concatenate([jnp.zeros(((window_blocks - 1) * tok_rows, 2 * AD), jnp.bfloat16), kv_send], 0)

        def attend_block(block_index, query16=query16, kv_front=kv_front):
            start_row = block_index * tok_rows
            query_rows = lax.dynamic_slice_in_dim(query16, start_row, tok_rows)
            window = lax.dynamic_slice_in_dim(kv_front, start_row, window_blocks * tok_rows)
            return attend(query_rows, window, attention_keep(start_row))
        attn_blocks, log_sums = lax.map(attend_block, jnp.arange(block_count, dtype=jnp.int32))
        attn_flat = attn_blocks.reshape(TOKENS, q_heads * AD)
        ao_weight = w_ao[attn_low:attn_low + q_heads * AD]
        attn_total = attn_total + jnp.dot(attn_flat, ao_weight, preferred_element_type=jnp.float32)
        saved.append(dict(zx_weight=zx_weight, dt_weight=dt_weight, gate_z=gate_z, dt_raw=dt_raw, ext_x=ext_x, conv_weight_x=conv_weight_x, pre_x=pre_x, rate=rate, skip_gain=skip_gain, pieces=pieces, states_in=states_in, ssd_y=ssd_y, silu_z=silu_z, gated=gated, gain_part=gain_part, mamba_in=mamba_in, mout_weight=mout_weight, q_weight=q_weight, kv_weight=kv_weight, query16=query16, kv_front=kv_front, attn_blocks=attn_blocks, log_sums=log_sums, attn_flat=attn_flat, ao_weight=ao_weight))
    mamba_scale = lax.rsqrt(square_total / MI + epsilon)[:, None]
    hidden_one = x_float + mamba_multiplier * mamba_scale * mamba_total + attention_multiplier * attn_total
    norm_two = lax.rsqrt(lax.optimization_barrier(jnp.mean(hidden_one * hidden_one, axis=-1, keepdims=True)) + epsilon)
    normed_two = (hidden_one * norm_two * norm2_gain).astype(jnp.bfloat16)
    gate_pre = jnp.dot(normed_two, w_gu[:, 0, :], preferred_element_type=jnp.float32) * gate_multiplier
    up_proj = jnp.dot(normed_two, w_gu[:, 1, :], preferred_element_type=jnp.float32)
    gate_act = jax.nn.silu(gate_pre)
    ff_hidden = (gate_act * up_proj).astype(jnp.bfloat16)
    output = (hidden_one + down_multiplier * jnp.dot(ff_hidden, w_down, preferred_element_type=jnp.float32)).astype(jnp.bfloat16)
    grad_out = cotangent.astype(jnp.float32)
    grad_ff = (down_multiplier * grad_out).astype(jnp.bfloat16)
    grad_down = product_t(ff_hidden, grad_ff)
    grad_hidden = jnp.dot(grad_ff, w_down.T, preferred_element_type=jnp.float32)
    silu_slope = silu_grad(gate_pre)
    grad_gate16 = (grad_hidden * up_proj * silu_slope * gate_multiplier).astype(jnp.bfloat16)
    grad_up16 = (grad_hidden * gate_act).astype(jnp.bfloat16)
    grad_gu = jnp.stack([product_t(normed_two, grad_gate16), product_t(normed_two, grad_up16)], axis=1)
    grad_normed_two = jnp.dot(grad_gate16, w_gu[:, 0, :].T, preferred_element_type=jnp.float32) + jnp.dot(grad_up16, w_gu[:, 1, :].T, preferred_element_type=jnp.float32)
    scaled_two = grad_normed_two * norm2_gain
    grad_gain_two = lax.optimization_barrier(jnp.sum(grad_normed_two * hidden_one * norm_two, axis=0))
    grad_hidden_one = grad_out + norm_two * scaled_two - hidden_one * norm_two ** 3 * lax.optimization_barrier(jnp.mean(scaled_two * hidden_one, axis=-1, keepdims=True))
    grad_mamba16 = (mamba_multiplier * mamba_scale * grad_hidden_one).astype(jnp.bfloat16)
    grad_scale = mamba_multiplier * lax.optimization_barrier(jnp.sum(grad_hidden_one * mamba_total, axis=-1, keepdims=True))
    grad_attn16 = (attention_multiplier * grad_hidden_one).astype(jnp.bfloat16)
    grad_normed = jnp.zeros((TOKENS, D), jnp.float32)
    grad_bc_total = jnp.zeros((D, 2 * NS), jnp.float32)
    grad_conv_bc = jnp.zeros((tap_count, 2 * NS), jnp.float32)
    zx_parts, dt_parts, mout_parts, q_parts, kv_parts, ao_parts = ([], [], [], [], [], [])
    mnorm_parts, conv_x_parts, bias_parts, skip_parts = ([], [], [], [])
    for group_index in range(group_count):
        saved_group = saved[group_index]
        mout_parts.append(product_t(saved_group['mamba_in'], grad_mamba16))
        grad_mamba_in = jnp.dot(grad_mamba16, saved_group['mout_weight'].T, preferred_element_type=jnp.float32)
        gated = saved_group['gated']
        mnorm_parts.append(lax.optimization_barrier(jnp.sum(grad_mamba_in * gated, axis=0)))
        grad_gated = saved_group['gain_part'] * grad_mamba_in - grad_scale * mamba_scale ** 3 * gated / MI
        grad_ssd_y = grad_gated * saved_group['silu_z']
        grad_z = grad_gated * saved_group['ssd_y'] * silu_grad(saved_group['gate_z'])
        skip_gain = saved_group['skip_gain']
        back_pieces = saved_group['pieces'] + (saved_group['states_in'], grad_ssd_y.reshape(block_count, tok_rows, inner_half))

        def backward_block(grad_state, block_pieces, skip_gain=skip_gain):
            block_xs, block_b, block_c, block_log, block_step, block_pair, block_first, block_last, block_state, block_grad = block_pieces

            def out_part(chan_in, b_in, c_in, log_in, step_in, state_given, skip_in):
                return ssd_out(chan_in, b_in, c_in, log_in, step_in, state_given, skip_in, block_pair, block_first)
            _, pull_out = jax.vjp(out_part, block_xs, block_b, block_c, block_log, block_step, block_state, skip_gain)
            grad_xs_one, grad_b_one, grad_c_one, grad_log_one, grad_step_one, grad_state_one, grad_skip_one = pull_out(block_grad)

            def end_part(chan_in, b_in, log_in, step_in, state_given):
                return ssd_end(chan_in, b_in, log_in, step_in, state_given, block_first, block_last)[0]
            _, pull_end = jax.vjp(end_part, block_xs, block_b, block_log, block_step, block_state)
            grad_xs_two, grad_b_two, grad_log_two, grad_step_two, grad_state_two = pull_end(grad_state)
            return (grad_state_one + grad_state_two, (grad_xs_one + grad_xs_two, grad_b_one + grad_b_two, grad_c_one, grad_log_one + grad_log_two, grad_step_one + grad_step_two, grad_skip_one))
        zero_state = jnp.zeros((heads_here, MP, NS), jnp.float32)
        _, block_grads = lax.scan(backward_block, zero_state, back_pieces, reverse=True)
        grad_xs = block_grads[0].reshape(TOKENS, inner_half)
        grad_b = block_grads[1].reshape(TOKENS, NS)
        grad_c = block_grads[2].reshape(TOKENS, NS)
        grad_log = block_grads[3].reshape(TOKENS, heads_here)
        grad_step = block_grads[4].reshape(TOKENS, heads_here) + grad_log * saved_group['rate'][None, :]
        skip_parts.append(lax.optimization_barrier(jnp.sum(block_grads[5], axis=0)))
        grad_dt_raw = grad_step * jax.nn.sigmoid(saved_group['dt_raw'])
        bias_parts.append(lax.optimization_barrier(jnp.sum(grad_dt_raw, axis=0)))
        grad_pre_x = grad_xs * silu_grad(saved_group['pre_x'])
        grad_pre_bc = jnp.concatenate([grad_b, grad_c], axis=-1) * silu_grad(pre_bc)
        grad_ext_x, grad_conv_x_part = conv_grads(saved_group['ext_x'], conv_keeps, saved_group['conv_weight_x'], grad_pre_x)
        grad_ext_bc, grad_conv_bc_part = conv_grads(ext_bc, conv_keeps, conv_bc, grad_pre_bc)
        conv_x_parts.append(grad_conv_x_part)
        grad_conv_bc = grad_conv_bc + grad_conv_bc_part
        grad_zx16 = jnp.concatenate([grad_z, grad_ext_x[tap_count - 1:]], axis=-1).astype(jnp.bfloat16)
        grad_bc16 = grad_ext_bc[tap_count - 1:].astype(jnp.bfloat16)
        grad_dt16 = grad_dt_raw.astype(jnp.bfloat16)
        zx_parts.append(product_t(normed, grad_zx16).reshape(D, 2, inner_half))
        grad_bc_total = grad_bc_total + product_t(normed, grad_bc16)
        dt_parts.append(product_t(normed, grad_dt16))
        grad_normed = grad_normed + jnp.dot(grad_zx16, saved_group['zx_weight'].T, preferred_element_type=jnp.float32) + jnp.dot(grad_bc16, w_bc.T, preferred_element_type=jnp.float32) + jnp.dot(grad_dt16, saved_group['dt_weight'].T, preferred_element_type=jnp.float32)
        ao_parts.append(product_t(saved_group['attn_flat'], grad_attn16))
        grad_heads16 = jnp.dot(grad_attn16, saved_group['ao_weight'].T, preferred_element_type=jnp.float32).astype(jnp.bfloat16).reshape(block_count, tok_rows, q_heads, AD)
        query16 = saved_group['query16']
        kv_front = saved_group['kv_front']

        def back_block(buffer, block_pieces, query16=query16, kv_front=kv_front):
            block_index, block_log, block_out, block_grad = block_pieces
            start_row = block_index * tok_rows
            query_rows = lax.dynamic_slice_in_dim(query16, start_row, tok_rows)
            window = lax.dynamic_slice_in_dim(kv_front, start_row, window_blocks * tok_rows)
            grad_query, grad_window = attend_back(query_rows, window, attention_keep(start_row), block_log, block_out, block_grad)
            current = lax.dynamic_slice_in_dim(buffer, start_row, window_blocks * tok_rows) + grad_window
            return (lax.dynamic_update_slice_in_dim(buffer, current, start_row, 0), grad_query)
        buffer_init = jnp.zeros(((window_blocks - 1) * tok_rows + TOKENS, 2 * AD), jnp.float32)
        buffer, grad_query_blocks = lax.scan(back_block, buffer_init, (jnp.arange(block_count, dtype=jnp.int32), saved_group['log_sums'], saved_group['attn_blocks'], grad_heads16))
        grad_kv_own = buffer[(window_blocks - 1) * tok_rows:]
        grad_query = grad_query_blocks.reshape(TOKENS, q_heads, AD)
        grad_q16 = rotate(grad_query, positions, -1.0).reshape(TOKENS, q_heads * AD).astype(jnp.bfloat16)
        grad_key = rotate(grad_kv_own[:, None, :AD], positions, -1.0)[:, 0, :] * key_multiplier
        grad_kv16 = jnp.concatenate([grad_key, grad_kv_own[:, AD:]], axis=-1).astype(jnp.bfloat16)
        q_parts.append(product_t(normed, grad_q16))
        kv_parts.append(product_t(normed, grad_kv16).reshape(D, 2, AD))
        grad_normed = grad_normed + jnp.dot(grad_q16, saved_group['q_weight'].T, preferred_element_type=jnp.float32) + jnp.dot(grad_kv16, saved_group['kv_weight'].T, preferred_element_type=jnp.float32)
    scaled_one = grad_normed * norm1_gain
    grad_gain_one = lax.optimization_barrier(jnp.sum(grad_normed * x_float * norm_one, axis=0))
    x_grad = grad_hidden_one + norm_one * scaled_one - x_float * norm_one ** 3 * lax.optimization_barrier(jnp.mean(scaled_one * x_float, axis=-1, keepdims=True))
    return (output, x_grad, jnp.concatenate(zx_parts, axis=2), grad_bc_total, jnp.concatenate(dt_parts, axis=1), jnp.concatenate(mout_parts, axis=0), jnp.concatenate(q_parts, axis=1), jnp.concatenate(kv_parts, axis=2), jnp.concatenate(ao_parts, axis=0), grad_gu, grad_down, grad_gain_one, grad_gain_two, jnp.concatenate(mnorm_parts, axis=0), jnp.concatenate(conv_x_parts, axis=1), grad_conv_bc, jnp.concatenate(bias_parts, axis=0), jnp.concatenate(skip_parts, axis=0))
```

```python
import jax
import jax.numpy as jnp
from jax import lax
from jax.sharding import PartitionSpec as P

MI = 1536
MP = 64
NS = 128
AD = 64
TOK_DEV = 176


epsilon = 1e-05
key_multiplier = 0.390625
attention_multiplier = 0.9375
mamba_multiplier = 0.5
gate_multiplier = 0.75
down_multiplier = 0.5
rope_base = 100000000000.0
far_below = -1e30
highest = lax.Precision.HIGHEST
group_blocks = 4


def from_behind(block, axis, distance):
    devices = range(lax.axis_size(axis))
    route = [(i - distance, i) for i in devices if i - distance in devices]
    return lax.ppermute(block, axis, route)


def gather_states(carry, end):
    heads = end.shape[0]
    packed = jnp.concatenate(
        [end.reshape(heads, -1), jnp.broadcast_to(carry[:, None], (heads, end.shape[2]))], axis=1
    )
    gathered = lax.all_gather(packed, "seq")
    ends = gathered[:, :, : end.shape[1] * end.shape[2]].reshape((-1,) + end.shape)
    return (gathered[:, :, -1], ends)


def entering(carries, ends, reverse):
    count = lax.axis_size("seq")
    place = lax.axis_index("seq")
    ahead = count - 1 - place if reverse else place
    if reverse:
        carries, ends = (carries[::-1], ends[::-1])
    hops = jnp.arange(count, dtype=jnp.int32)
    between = (hops[None, :] > hops[:, None]) & (hops[None, :] < ahead)
    weights = jnp.prod(jnp.where(between[:, :, None], carries[None], 1.0), axis=1)
    weights = jnp.where((hops < ahead)[:, None], weights, 0.0)
    return jnp.sum(weights[:, :, None, None] * ends, axis=0)


def head_sum(part):
    count = lax.axis_size("head")
    total = part.astype(jnp.float32)
    if count != 2:
        return lax.psum(total, "head")
    return total + lax.ppermute(part, "head", [(0, 1), (1, 0)]).astype(jnp.float32)


def seq_sum(part):
    count = lax.axis_size("seq")
    if count & (count - 1):
        return lax.psum(part, "seq")
    distance = 1
    while distance < count:
        part = part + lax.ppermute(part, "seq", [(i, i ^ distance) for i in range(count)])
        distance = distance * 2
    return part


def silu_grad(values):
    sigmoid_value = jax.nn.sigmoid(values)
    return sigmoid_value * (1.0 + values * (1.0 - sigmoid_value))


def rotate(values, positions, direction):
    half_dim = values.shape[-1] // 2
    frequency = jnp.power(
        jnp.float32(rope_base), -jnp.arange(half_dim, dtype=jnp.float32) / half_dim
    )
    angles = positions.astype(jnp.float32)[:, None] * frequency[None, :]
    cosine = jnp.cos(angles)[:, None, :]
    sine_part = direction * jnp.sin(angles)[:, None, :]
    first_half = values[..., :half_dim]
    second_half = values[..., half_dim:]
    return jnp.concatenate(
        [
            first_half * cosine - second_half * sine_part,
            second_half * cosine + first_half * sine_part,
        ],
        axis=-1,
    )


def conv_masks(conv_seg, tap_count):
    row_count = conv_seg.shape[0] - tap_count + 1
    own_seg = conv_seg[tap_count - 1 :]
    return [
        conv_seg[tap_index : tap_index + row_count] == own_seg for tap_index in range(tap_count)
    ]


def conv_apply(extended, keep_list, weight):
    row_count = keep_list[0].shape[0]
    result = jnp.zeros((row_count, extended.shape[1]), jnp.float32)
    for tap_index in range(weight.shape[0]):
        result = result + weight[tap_index][None, :] * jnp.where(
            keep_list[tap_index][:, None], extended[tap_index : tap_index + row_count], 0.0
        )
    return result


def conv_grads(extended, keep_list, weight, grad_pre):
    row_count = grad_pre.shape[0]
    grad_ext = jnp.zeros(extended.shape, jnp.float32)
    weight_parts = []
    for tap_index in range(weight.shape[0]):
        masked = jnp.where(keep_list[tap_index][:, None], grad_pre, 0.0)
        grad_ext = grad_ext.at[tap_index : tap_index + row_count].add(
            weight[tap_index][None, :] * masked
        )
        weight_parts.append(jnp.sum(masked * extended[tap_index : tap_index + row_count], axis=0))
    return (grad_ext, jnp.stack(weight_parts))


def lower_ones(row_count):
    row_ids = jnp.arange(row_count, dtype=jnp.int32)
    return (row_ids[:, None] >= row_ids[None, :]).astype(jnp.float32)


def ssd_out(
    channels, b_matrix, c_matrix, log_decay, step_size, state_in, skip_gain, pair_keep, first_keep
):
    row_count, head_count = log_decay.shape
    cumulative = jnp.dot(lower_ones(row_count), log_decay, precision=highest)
    cum_heads = cumulative.T
    difference = cum_heads[:, :, None] - cum_heads[:, None, :]
    decay_matrix = jnp.where(
        pair_keep[None], jnp.exp(jnp.where(pair_keep[None], difference, 0.0)), 0.0
    )
    inner_product = jnp.dot(c_matrix, b_matrix.T, precision=highest)
    mixing = decay_matrix * inner_product[None]
    inputs = channels.reshape(row_count, head_count, -1)
    scaled = inputs * step_size[:, :, None]
    result = jnp.einsum("hts,shp->thp", mixing, scaled, precision=highest)
    carried = jnp.einsum("tn,hpn->thp", c_matrix, state_in, precision=highest)
    result = (
        result
        + (jnp.exp(cumulative) * first_keep[:, None])[:, :, None] * carried
        + skip_gain[None, :, None] * inputs
    )
    return result.reshape(row_count, -1)


def ssd_end(channels, b_matrix, log_decay, step_size, state_in, first_keep, last_keep):
    row_count, head_count = log_decay.shape
    cumulative = jnp.dot(lower_ones(row_count), log_decay, precision=highest)
    whole_sum = cumulative[-1]
    tail_decay = jnp.exp(whole_sum[None, :] - cumulative) * last_keep[:, None]
    scaled = channels.reshape(row_count, head_count, -1) * (step_size * tail_decay)[:, :, None]
    end_state = jnp.einsum("thp,tn->hpn", scaled, b_matrix, precision=highest)
    carry_factor = jnp.exp(whole_sum) * first_keep[-1]
    return (end_state + carry_factor[:, None, None] * state_in, carry_factor)


def step_plan(reach_blocks):
    plan_list = []
    held_blocks = 1
    while held_blocks < reach_blocks:
        extra_blocks = min(held_blocks, reach_blocks - held_blocks)
        plan_list.append((held_blocks, extra_blocks))
        held_blocks = held_blocks + extra_blocks
    return plan_list


def double_window(kv_send, reach_blocks, tok_rows):
    held = kv_send
    for held_blocks, extra_blocks in step_plan(reach_blocks):
        arrived = from_behind(held[(held_blocks - extra_blocks) * tok_rows :], "seq", held_blocks)
        held = jnp.concatenate([arrived, held], 0)
    return held


def double_back(window_grads, reach_blocks, tok_rows):
    running = window_grads
    for held_blocks, extra_blocks in reversed(step_plan(reach_blocks)):
        arrived_part = running[: extra_blocks * tok_rows]
        kept_part = running[extra_blocks * tok_rows :]
        returned = from_behind(arrived_part.astype(jnp.bfloat16), "seq", -held_blocks).astype(
            arrived_part.dtype
        )
        running = kept_part.at[(held_blocks - extra_blocks) * tok_rows :].add(returned)
    return running


def attend(query_rows, window_kv, keep_mask, group_rows, group_total):
    q_heads = query_rows.shape[1]
    tok_rows = query_rows.shape[0]
    top_init = jnp.full((q_heads, tok_rows, 1), far_below, jnp.float32)
    total_init = jnp.zeros((q_heads, tok_rows, 1), jnp.float32)

    def group_scores(group_index):
        start = group_index * group_rows
        group_kv = lax.dynamic_slice_in_dim(window_kv, start, group_rows)
        group_mask = lax.dynamic_slice_in_dim(keep_mask, start, group_rows, 1)
        scores = jnp.einsum(
            "tgd,kd->gtk", query_rows, group_kv[:, :AD], preferred_element_type=jnp.float32
        ) * AD ** (-0.5)
        return (scores, group_kv, group_mask)

    def first_pass(group_index, carried):

        def first_live(state):
            row_top, total = state
            scores, _, group_mask = group_scores(group_index)
            masked = jnp.where(group_mask[None], scores, far_below)
            new_top = jnp.maximum(row_top, jnp.max(masked, axis=-1, keepdims=True))
            new_total = total * jnp.exp(row_top - new_top) + jnp.sum(
                jnp.exp(masked - new_top), axis=-1, keepdims=True
            )
            return (new_top, new_total)

        mask_here = lax.dynamic_slice_in_dim(keep_mask, group_index * group_rows, group_rows, 1)
        return lax.cond(jnp.any(mask_here), first_live, lambda state: state, carried)

    row_top, total = lax.fori_loop(0, group_total, first_pass, (top_init, total_init))
    log_sum = row_top + jnp.log(total)

    def second_pass(group_index, acc):

        def second_live(acc_in):
            scores, group_kv, group_mask = group_scores(group_index)
            probabilities = jnp.exp(
                jnp.where(group_mask[None], scores - log_sum, far_below)
            ).astype(jnp.bfloat16)
            return acc_in + jnp.einsum(
                "gtk,kd->tgd", probabilities, group_kv[:, AD:], preferred_element_type=jnp.float32
            )

        mask_here = lax.dynamic_slice_in_dim(keep_mask, group_index * group_rows, group_rows, 1)
        return lax.cond(jnp.any(mask_here), second_live, lambda acc_in: acc_in, acc)

    result = lax.fori_loop(
        0, group_total, second_pass, jnp.zeros((tok_rows, q_heads, AD), jnp.float32)
    )
    return (result.astype(jnp.bfloat16), log_sum)


def attend_back(query_rows, window_kv, keep_mask, log_sum, out_rows, grad_rows):
    key_rows = window_kv[:, :AD]
    value_rows = window_kv[:, AD:]
    scores = jnp.einsum(
        "tgd,kd->gtk", query_rows, key_rows, preferred_element_type=jnp.float32
    ) * AD ** (-0.5)
    probabilities = jnp.exp(jnp.where(keep_mask[None], scores - log_sum, far_below))
    row_delta = jnp.sum(grad_rows.astype(jnp.float32) * out_rows.astype(jnp.float32), axis=-1).T
    grad_probs = jnp.einsum(
        "tgd,kd->gtk", grad_rows, value_rows, preferred_element_type=jnp.float32
    )
    grad_scores = (probabilities * (grad_probs - row_delta[:, :, None])).astype(jnp.bfloat16)
    probs_rounded = probabilities.astype(jnp.bfloat16)
    grad_query = jnp.einsum(
        "gtk,kd->tgd", grad_scores, key_rows, preferred_element_type=jnp.float32
    ) * AD ** (-0.5)
    grad_keys = jnp.einsum(
        "gtk,tgd->kd", grad_scores, query_rows, preferred_element_type=jnp.float32
    ) * AD ** (-0.5)
    grad_values = jnp.einsum(
        "gtk,tgd->kd", probs_rounded, grad_rows, preferred_element_type=jnp.float32
    )
    return (grad_query, jnp.concatenate([grad_keys, grad_values], axis=-1))


def column_ends(parts):
    ends = []
    for part in parts[:-1]:
        ends.append(part.shape[1] + (ends[-1] if ends else 0))
    return ends


def times_rows(left, right):
    return jnp.einsum("tc,dc->td", left, right, preferred_element_type=jnp.float32)


def scatter_sum(parts):
    packed = jnp.concatenate([part.astype(jnp.bfloat16) for part in parts], axis=1)
    return lax.psum_scatter(packed, "seq", scatter_dimension=0, tiled=True).astype(jnp.float32)


def product_t(left, right):
    return jnp.einsum("tc,td->cd", left, right, preferred_element_type=jnp.float32)


def local(
    x_in,
    seg_ids,
    decay_exp,
    cotangent,
    w_zx,
    w_bc,
    w_dt,
    w_mout,
    w_q,
    w_kv,
    w_ao,
    w_gu,
    w_down,
    norm1_gain,
    norm2_gain,
    mnorm_gain,
    conv_x,
    conv_bc,
    dt_bias,
    skip_d,
):
    tok_rows = x_in.shape[0]
    seq_count = lax.axis_size("seq")
    reach_blocks = tok_rows * seq_count * 3 // 4 // tok_rows + 1
    window_blocks = (reach_blocks + group_blocks - 1) // group_blocks * group_blocks
    lead_blocks = window_blocks - reach_blocks
    group_total = window_blocks // group_blocks
    group_rows = group_blocks * tok_rows
    tap_count = conv_x.shape[0]
    pad_rows = window_blocks * tok_rows
    seq_index = lax.axis_index("seq")
    start_row = seq_index * tok_rows
    token_ids = jnp.arange(tok_rows, dtype=jnp.int32)
    positions = start_row + token_ids
    seg_front = jnp.concatenate([jnp.full((pad_rows,), -1, jnp.int32), seg_ids])
    own_seg = lax.dynamic_slice_in_dim(seg_front, start_row + pad_rows, tok_rows)
    conv_seg = lax.dynamic_slice_in_dim(
        seg_front, start_row + pad_rows - tap_count + 1, tok_rows + tap_count - 1
    )
    key_seg = lax.dynamic_slice_in_dim(seg_front, start_row + tok_rows, window_blocks * tok_rows)
    prev_seg = conv_seg[tap_count - 2]
    pair_keep = (token_ids[:, None] >= token_ids[None, :]) & (own_seg[:, None] == own_seg[None, :])
    first_keep = (own_seg == prev_seg).astype(jnp.float32)
    last_keep = (own_seg == own_seg[-1]).astype(jnp.float32)
    conv_keeps = conv_masks(conv_seg, tap_count)
    key_pos = (
        start_row
        - (window_blocks - 1) * tok_rows
        + jnp.arange(window_blocks * tok_rows, dtype=jnp.int32)
    )
    attn_keep = (key_pos[None, :] <= positions[:, None]) & (key_seg[None, :] == own_seg[:, None])
    shard_rows, _, inner_half = w_zx.shape
    ff_half = w_gu.shape[2]
    heads_here = w_dt.shape[1]
    width = x_in.shape[1]
    q_width = w_q.shape[1]
    in_parts = (w_zx.reshape(shard_rows, -1), w_bc, w_q, w_kv.reshape(shard_rows, -1), w_dt)
    out_parts = (w_mout.T, w_ao.T)
    ff_parts = (w_gu.reshape(shard_rows, -1), w_down.T)
    in_full, out_full, ff_full = [
        lax.all_gather(jnp.concatenate(parts, axis=1), "seq", axis=0, tiled=True)
        for parts in (in_parts, out_parts, ff_parts)
    ]
    in_ends = column_ends(in_parts)
    mout_full, attn_out_full = jnp.split(out_full, column_ends(out_parts), axis=1)
    gateup_full, down_full = jnp.split(ff_full, column_ends(ff_parts), axis=1)
    x_float = x_in.astype(jnp.float32)
    norm_one = lax.rsqrt(jnp.mean(x_float * x_float, axis=-1, keepdims=True) + epsilon)
    normed = (x_float * norm_one * norm1_gain).astype(jnp.bfloat16)
    zx_proj, bc_proj, q_proj, keyval, dt_proj = jnp.split(
        jnp.dot(normed, in_full, preferred_element_type=jnp.float32), in_ends, axis=1
    )
    gate_z = zx_proj[:, :inner_half]
    x_send = zx_proj[:, inner_half:].astype(jnp.bfloat16)
    bc_send = bc_proj.astype(jnp.bfloat16)
    dt_raw = dt_proj + dt_bias
    edge_x, edge_bc = from_behind(
        (x_send[tok_rows - tap_count + 1 :], bc_send[tok_rows - tap_count + 1 :]), "seq", 1
    )
    ext_x = jnp.concatenate([edge_x, x_send], 0).astype(jnp.float32)
    ext_bc = jnp.concatenate([edge_bc, bc_send], 0).astype(jnp.float32)
    pre_x = conv_apply(ext_x, conv_keeps, conv_x)
    pre_bc = conv_apply(ext_bc, conv_keeps, conv_bc)
    conv_xs = jax.nn.silu(pre_x)
    conv_bcs = jax.nn.silu(pre_bc)
    b_matrix = conv_bcs[:, :NS]
    c_matrix = conv_bcs[:, NS:]
    step_size = jax.nn.softplus(dt_raw)
    rate = -jnp.exp2(-decay_exp.astype(jnp.float32)) * (256.0 / TOK_DEV)
    log_decay = step_size * rate[None, :]
    zero_state = jnp.zeros((heads_here, MP, NS), jnp.float32)
    local_end, local_carry = ssd_end(
        conv_xs, b_matrix, log_decay, step_size, zero_state, first_keep, last_keep
    )
    carries, ends = gather_states(local_carry, local_end)
    state_in = entering(carries, ends, False)
    ssd_y = ssd_out(
        conv_xs, b_matrix, c_matrix, log_decay, step_size, state_in, skip_d, pair_keep, first_keep
    )
    silu_z = jax.nn.silu(gate_z)
    gated = ssd_y * silu_z
    square_part = jnp.sum(gated * gated, axis=-1)
    mamba_in = (gated * mnorm_gain).astype(jnp.bfloat16)
    mamba_part = times_rows(mamba_in, mout_full)
    q_heads = q_width // AD
    query_raw = q_proj.reshape(tok_rows, q_heads, AD)
    query16 = rotate(query_raw, positions, 1.0).astype(jnp.bfloat16)
    key_rot = rotate(keyval[:, None, :AD] * key_multiplier, positions, 1.0)[:, 0, :]
    kv_send = jnp.concatenate([key_rot, keyval[:, AD:]], axis=-1).astype(jnp.bfloat16)
    reached = double_window(kv_send, reach_blocks, tok_rows)
    window_flat = jnp.concatenate(
        [jnp.zeros((lead_blocks * tok_rows, 2 * AD), jnp.bfloat16), reached], 0
    )
    attn_out16, log_sum = attend(query16, window_flat, attn_keep, group_rows, group_total)
    attn_flat = attn_out16.reshape(tok_rows, q_heads * AD)
    attn_part = times_rows(attn_flat, attn_out_full)
    square_sum = head_sum(square_part)
    mamba_sum = head_sum(mamba_part)
    attn_sum = head_sum(attn_part)
    mamba_scale = lax.rsqrt(square_sum / MI + epsilon)[:, None]
    hidden_one = (
        x_float + mamba_multiplier * mamba_scale * mamba_sum + attention_multiplier * attn_sum
    )
    norm_two = lax.rsqrt(jnp.mean(hidden_one * hidden_one, axis=-1, keepdims=True) + epsilon)
    normed_two = (hidden_one * norm_two * norm2_gain).astype(jnp.bfloat16)
    gateup = jnp.dot(normed_two, gateup_full, preferred_element_type=jnp.float32)
    gate_pre = gateup[:, :ff_half] * gate_multiplier
    up_proj = gateup[:, ff_half:]
    gate_act = jax.nn.silu(gate_pre)
    ff_hidden = (gate_act * up_proj).astype(jnp.bfloat16)
    ff_part = times_rows(ff_hidden, down_full)
    ff_sum = head_sum(ff_part.astype(jnp.bfloat16))
    output = (hidden_one + down_multiplier * ff_sum).astype(jnp.bfloat16)
    grad_out = cotangent.astype(jnp.float32)
    grad_ff = (down_multiplier * grad_out).astype(jnp.bfloat16)
    grad_hidden = jnp.dot(grad_ff, down_full, preferred_element_type=jnp.float32)
    silu_slope = silu_grad(gate_pre)
    grad_gateup = jnp.concatenate(
        [grad_hidden * up_proj * silu_slope * gate_multiplier, grad_hidden * gate_act], axis=-1
    ).astype(jnp.bfloat16)
    grad_two_part = times_rows(grad_gateup, gateup_full)
    grad_normed_two = head_sum(grad_two_part)
    ff_shard = scatter_sum((product_t(normed_two, grad_gateup), product_t(grad_ff, ff_hidden)))
    shard_gu = ff_shard[:, : 2 * ff_half].reshape(shard_rows, 2, ff_half)
    shard_down = ff_shard[:, 2 * ff_half :].T
    scaled_two = grad_normed_two * norm2_gain
    grad_gain_two = jnp.sum(grad_normed_two * hidden_one * norm_two, axis=0)
    grad_hidden_one = (
        grad_out
        + norm_two * scaled_two
        - hidden_one * norm_two**3 * jnp.mean(scaled_two * hidden_one, axis=-1, keepdims=True)
    )
    grad_mamba16 = (mamba_multiplier * mamba_scale * grad_hidden_one).astype(jnp.bfloat16)
    grad_scale = mamba_multiplier * jnp.sum(grad_hidden_one * mamba_sum, axis=-1, keepdims=True)
    grad_attn16 = (attention_multiplier * grad_hidden_one).astype(jnp.bfloat16)
    out_shard = scatter_sum((product_t(grad_mamba16, mamba_in), product_t(grad_attn16, attn_flat)))
    shard_mout = out_shard[:, :inner_half].T
    shard_ao = out_shard[:, inner_half:].T
    grad_mamba_in = jnp.dot(grad_mamba16, mout_full, preferred_element_type=jnp.float32)
    grad_mnorm = jnp.sum(grad_mamba_in * gated, axis=0)
    grad_gated = mnorm_gain * grad_mamba_in - grad_scale * mamba_scale**3 * gated / MI
    grad_ssd_y = grad_gated * silu_z
    grad_z = grad_gated * ssd_y * silu_grad(gate_z)

    def out_part(chan_in, b_in, c_in, log_in, step_in, state_given, skip_in):
        return ssd_out(
            chan_in, b_in, c_in, log_in, step_in, state_given, skip_in, pair_keep, first_keep
        )

    _, pull_out = jax.vjp(
        out_part, conv_xs, b_matrix, c_matrix, log_decay, step_size, state_in, skip_d
    )
    (
        grad_xs_one,
        grad_b_one,
        grad_c_one,
        grad_log_one,
        grad_step_one,
        grad_state_local,
        grad_skip,
    ) = pull_out(grad_ssd_y)
    grad_state_end = entering(carries, lax.all_gather(grad_state_local, "seq"), True)

    def end_part(chan_in, b_in, log_in, step_in):
        return ssd_end(chan_in, b_in, log_in, step_in, state_in, first_keep, last_keep)[0]

    _, pull_end = jax.vjp(end_part, conv_xs, b_matrix, log_decay, step_size)
    grad_xs_two, grad_b_two, grad_log_two, grad_step_two = pull_end(grad_state_end)
    grad_step = grad_step_one + grad_step_two + (grad_log_one + grad_log_two) * rate[None, :]
    grad_dt_raw = grad_step * jax.nn.sigmoid(dt_raw)
    grad_dt_bias = jnp.sum(grad_dt_raw, axis=0)
    grad_pre_x = (grad_xs_one + grad_xs_two) * silu_grad(pre_x)
    grad_pre_bc = jnp.concatenate([grad_b_one + grad_b_two, grad_c_one], axis=-1) * silu_grad(
        pre_bc
    )
    grad_ext_x, grad_conv_x = conv_grads(ext_x, conv_keeps, conv_x, grad_pre_x)
    grad_ext_bc, grad_conv_bc = conv_grads(ext_bc, conv_keeps, conv_bc, grad_pre_bc)
    back_x, back_bc = from_behind(
        (grad_ext_x[: tap_count - 1], grad_ext_bc[: tap_count - 1]), "seq", -1
    )
    grad_x_send = grad_ext_x[tap_count - 1 :].at[tok_rows - tap_count + 1 :].add(back_x)
    grad_bc_send = grad_ext_bc[tap_count - 1 :].at[tok_rows - tap_count + 1 :].add(back_bc)
    grad_zx16 = jnp.concatenate([grad_z, grad_x_send], axis=-1).astype(jnp.bfloat16)
    grad_bc16 = grad_bc_send.astype(jnp.bfloat16)
    grad_dt16 = grad_dt_raw.astype(jnp.bfloat16)
    grad_heads16 = (
        jnp.dot(grad_attn16, attn_out_full, preferred_element_type=jnp.float32)
        .astype(jnp.bfloat16)
        .reshape(tok_rows, q_heads, AD)
    )

    def back_group(group_index, carried):
        query_acc, window_grads = carried
        start = group_index * group_rows
        group_kv = lax.dynamic_slice_in_dim(window_flat, start, group_rows)
        group_mask = lax.dynamic_slice_in_dim(attn_keep, start, group_rows, 1)

        def back_live(unused):
            return attend_back(query16, group_kv, group_mask, log_sum, attn_out16, grad_heads16)

        def dead(unused):
            return (
                jnp.zeros((tok_rows, q_heads, AD), jnp.float32),
                jnp.zeros((group_rows, 2 * AD), jnp.float32),
            )

        part_query, part_window = lax.cond(jnp.any(group_mask), back_live, dead, 0)
        return (
            query_acc + part_query,
            lax.dynamic_update_slice_in_dim(window_grads, part_window, start, 0),
        )

    grad_query, grad_window = lax.fori_loop(
        0,
        group_total,
        back_group,
        (
            jnp.zeros((tok_rows, q_heads, AD), jnp.float32),
            jnp.zeros((window_blocks * tok_rows, 2 * AD), jnp.float32),
        ),
    )
    grad_kv_own = double_back(grad_window[lead_blocks * tok_rows :], reach_blocks, tok_rows)
    grad_q16 = (
        rotate(grad_query, positions, -1.0).reshape(tok_rows, q_heads * AD).astype(jnp.bfloat16)
    )
    grad_key = rotate(grad_kv_own[:, None, :AD], positions, -1.0)[:, 0, :] * key_multiplier
    grad_kv16 = jnp.concatenate([grad_key, grad_kv_own[:, AD:]], axis=-1).astype(jnp.bfloat16)
    grad_in16 = jnp.concatenate([grad_zx16, grad_bc16, grad_q16, grad_kv16, grad_dt16], axis=1)
    in_shard = scatter_sum((product_t(normed, grad_in16),))
    shard_zx, shard_bc_part, shard_q, shard_kv, shard_dt = jnp.split(in_shard, in_ends, axis=1)
    shard_zx = shard_zx.reshape(shard_rows, 2, inner_half)
    shard_kv = shard_kv.reshape(shard_rows, 2, -1)
    shard_bc = head_sum(shard_bc_part)
    grad_normed_sum = head_sum(times_rows(grad_in16, in_full).astype(jnp.bfloat16))
    scaled_one = grad_normed_sum * norm1_gain
    grad_gain_one = jnp.sum(grad_normed_sum * x_float * norm_one, axis=0)
    x_grad = (
        grad_hidden_one
        + norm_one * scaled_one
        - x_float * norm_one**3 * jnp.mean(scaled_one * x_float, axis=-1, keepdims=True)
    )
    small_parts = (
        grad_gain_one,
        grad_gain_two,
        grad_mnorm,
        grad_conv_x,
        grad_conv_bc,
        grad_dt_bias,
        grad_skip,
    )
    small_sum = seq_sum(jnp.concatenate([part.reshape(-1) for part in small_parts]))
    small_out = []
    start = 0
    for part in small_parts:
        small_out.append(small_sum[start : start + part.size].reshape(part.shape))
        start = start + part.size
    sum_gain_one, sum_gain_two, sum_mnorm, sum_conv_x, conv_bc_part, sum_dt_bias, sum_skip = (
        small_out
    )
    sum_conv_bc = head_sum(conv_bc_part)
    return (
        output,
        x_grad,
        shard_zx,
        shard_bc,
        shard_dt,
        shard_mout,
        shard_q,
        shard_kv,
        shard_ao,
        shard_gu,
        shard_down,
        sum_gain_one,
        sum_gain_two,
        sum_mnorm,
        sum_conv_x,
        sum_conv_bc,
        sum_dt_bias,
        sum_skip,
    )


def solution(mesh):
    in_specs = (
        P("seq", None),
        P(),
        P("head"),
        P("seq", None),
        P("seq", None, "head"),
        P("seq", None),
        P("seq", "head"),
        P("head", "seq"),
        P("seq", "head"),
        P("seq", None, "head"),
        P("head", "seq"),
        P("seq", None, "head"),
        P("head", "seq"),
        P(),
        P(),
        P("head"),
        P(None, "head"),
        P(),
        P("head"),
        P("head"),
    )
    out_specs = (
        P("seq", None),
        P("seq", None),
        P("seq", None, "head"),
        P("seq", None),
        P("seq", "head"),
        P("head", "seq"),
        P("seq", "head"),
        P("seq", None, "head"),
        P("head", "seq"),
        P("seq", None, "head"),
        P("head", "seq"),
        P(),
        P(),
        P("head"),
        P(None, "head"),
        P(),
        P("head"),
        P("head"),
    )
    return jax.shard_map(local, mesh=mesh, in_specs=in_specs, out_specs=out_specs, check_vma=False)
```

```python
import jax
import jax.numpy as jnp
from jax import lax
from jax.sharding import PartitionSpec as P

MI = 1536
MP = 64
NS = 128
AD = 64
TOK_DEV = 176


epsilon = 1e-05
key_multiplier = 0.390625
attention_multiplier = 0.9375
mamba_multiplier = 0.5
gate_multiplier = 0.75
down_multiplier = 0.5
rope_base = 100000000000.0
far_below = -1e30
highest = lax.Precision.HIGHEST
group_blocks = 4


def from_behind(block, axis, distance):
    devices = range(lax.axis_size(axis))
    route = [(i - distance, i) for i in devices if i - distance in devices]
    return lax.ppermute(block, axis, route)


def entering(carry, end, reverse):
    heads, rows, columns = end.shape
    count = lax.axis_size("seq")
    sign = -1 if reverse else 1
    carry_part = jnp.broadcast_to(carry[:, None, None], (heads, 8, columns))
    held = from_behind(jnp.concatenate([end, carry_part], axis=1), "seq", sign)
    distance = 1
    while distance < count:
        arrived = from_behind(held, "seq", sign * distance)
        factor = held[:, rows : rows + 1]
        held = jnp.concatenate(
            [held[:, :rows] + factor * arrived[:, :rows], held[:, rows:] * arrived[:, rows:]],
            axis=1,
        )
        distance = distance * 2
    return held[:, :rows]


def head_sum(part):
    count = lax.axis_size("head")
    total = part.astype(jnp.float32)
    if count != 2:
        return lax.psum(total, "head")
    return total + lax.ppermute(part, "head", [(0, 1), (1, 0)]).astype(jnp.float32)


def seq_sum(part):
    count = lax.axis_size("seq")
    if count & (count - 1):
        return lax.psum(part, "seq")
    distance = 1
    while distance < count:
        part = part + lax.ppermute(part, "seq", [(i, i ^ distance) for i in range(count)])
        distance = distance * 2
    return part


def silu_grad(values):
    sigmoid_value = jax.nn.sigmoid(values)
    return sigmoid_value * (1.0 + values * (1.0 - sigmoid_value))


def rotate(values, positions, direction):
    half_dim = values.shape[-1] // 2
    frequency = jnp.power(
        jnp.float32(rope_base), -jnp.arange(half_dim, dtype=jnp.float32) / half_dim
    )
    angles = positions.astype(jnp.float32)[:, None] * frequency[None, :]
    cosine = jnp.cos(angles)[:, None, :]
    sine_part = direction * jnp.sin(angles)[:, None, :]
    first_half = values[..., :half_dim]
    second_half = values[..., half_dim:]
    return jnp.concatenate(
        [
            first_half * cosine - second_half * sine_part,
            second_half * cosine + first_half * sine_part,
        ],
        axis=-1,
    )


def conv_masks(conv_seg, tap_count):
    row_count = conv_seg.shape[0] - tap_count + 1
    own_seg = conv_seg[tap_count - 1 :]
    return [
        conv_seg[tap_index : tap_index + row_count] == own_seg for tap_index in range(tap_count)
    ]


def conv_apply(extended, keep_list, weight):
    row_count = keep_list[0].shape[0]
    result = jnp.zeros((row_count, extended.shape[1]), jnp.float32)
    for tap_index in range(weight.shape[0]):
        result = result + weight[tap_index][None, :] * jnp.where(
            keep_list[tap_index][:, None], extended[tap_index : tap_index + row_count], 0.0
        )
    return result


def conv_grads(extended, keep_list, weight, grad_pre):
    row_count = grad_pre.shape[0]
    grad_ext = jnp.zeros(extended.shape, jnp.float32)
    weight_parts = []
    for tap_index in range(weight.shape[0]):
        masked = jnp.where(keep_list[tap_index][:, None], grad_pre, 0.0)
        grad_ext = grad_ext.at[tap_index : tap_index + row_count].add(
            weight[tap_index][None, :] * masked
        )
        weight_parts.append(jnp.sum(masked * extended[tap_index : tap_index + row_count], axis=0))
    return (grad_ext, jnp.stack(weight_parts))


def lower_ones(row_count):
    row_ids = jnp.arange(row_count, dtype=jnp.int32)
    return (row_ids[:, None] >= row_ids[None, :]).astype(jnp.float32)


def ssd_out(
    channels, b_matrix, c_matrix, log_decay, step_size, state_in, skip_gain, pair_keep, first_keep
):
    row_count, head_count = log_decay.shape
    cumulative = jnp.dot(lower_ones(row_count), log_decay, precision=highest)
    cum_heads = cumulative.T
    difference = cum_heads[:, :, None] - cum_heads[:, None, :]
    decay_matrix = jnp.where(
        pair_keep[None], jnp.exp(jnp.where(pair_keep[None], difference, 0.0)), 0.0
    )
    inner_product = jnp.dot(c_matrix, b_matrix.T, precision=highest)
    mixing = decay_matrix * inner_product[None]
    inputs = channels.reshape(row_count, head_count, -1)
    scaled = inputs * step_size[:, :, None]
    result = jnp.einsum("hts,shp->thp", mixing, scaled, precision=highest)
    carried = jnp.einsum("tn,hpn->thp", c_matrix, state_in, precision=highest)
    result = (
        result
        + (jnp.exp(cumulative) * first_keep[:, None])[:, :, None] * carried
        + skip_gain[None, :, None] * inputs
    )
    return result.reshape(row_count, -1)


def ssd_end(channels, b_matrix, log_decay, step_size, state_in, first_keep, last_keep):
    row_count, head_count = log_decay.shape
    cumulative = jnp.dot(lower_ones(row_count), log_decay, precision=highest)
    whole_sum = cumulative[-1]
    tail_decay = jnp.exp(whole_sum[None, :] - cumulative) * last_keep[:, None]
    scaled = channels.reshape(row_count, head_count, -1) * (step_size * tail_decay)[:, :, None]
    end_state = jnp.einsum("thp,tn->hpn", scaled, b_matrix, precision=highest)
    carry_factor = jnp.exp(whole_sum) * first_keep[-1]
    return (end_state + carry_factor[:, None, None] * state_in, carry_factor)


def step_plan(reach_blocks):
    plan_list = []
    held_blocks = 1
    while held_blocks < reach_blocks:
        extra_blocks = min(held_blocks, reach_blocks - held_blocks)
        plan_list.append((held_blocks, extra_blocks))
        held_blocks = held_blocks + extra_blocks
    return plan_list


def double_window(kv_send, reach_blocks, tok_rows):
    held = kv_send
    for held_blocks, extra_blocks in step_plan(reach_blocks):
        arrived = from_behind(held[(held_blocks - extra_blocks) * tok_rows :], "seq", held_blocks)
        held = jnp.concatenate([arrived, held], 0)
    return held


def double_back(window_grads, reach_blocks, tok_rows):
    running = window_grads
    for held_blocks, extra_blocks in reversed(step_plan(reach_blocks)):
        arrived_part = running[: extra_blocks * tok_rows]
        kept_part = running[extra_blocks * tok_rows :]
        returned = from_behind(arrived_part.astype(jnp.bfloat16), "seq", -held_blocks).astype(
            arrived_part.dtype
        )
        running = kept_part.at[(held_blocks - extra_blocks) * tok_rows :].add(returned)
    return running


def attend(query_rows, window_kv, keep_mask, group_rows, group_total):
    q_heads = query_rows.shape[1]
    tok_rows = query_rows.shape[0]
    top_init = jnp.full((q_heads, tok_rows, 1), far_below, jnp.float32)
    total_init = jnp.zeros((q_heads, tok_rows, 1), jnp.float32)

    def group_scores(group_index):
        start = group_index * group_rows
        group_kv = lax.dynamic_slice_in_dim(window_kv, start, group_rows)
        group_mask = lax.dynamic_slice_in_dim(keep_mask, start, group_rows, 1)
        scores = jnp.einsum(
            "tgd,kd->gtk", query_rows, group_kv[:, :AD], preferred_element_type=jnp.float32
        ) * AD ** (-0.5)
        return (scores, group_kv, group_mask)

    def first_pass(group_index, carried):

        def first_live(state):
            row_top, total = state
            scores, _, group_mask = group_scores(group_index)
            masked = jnp.where(group_mask[None], scores, far_below)
            new_top = jnp.maximum(row_top, jnp.max(masked, axis=-1, keepdims=True))
            new_total = total * jnp.exp(row_top - new_top) + jnp.sum(
                jnp.exp(masked - new_top), axis=-1, keepdims=True
            )
            return (new_top, new_total)

        mask_here = lax.dynamic_slice_in_dim(keep_mask, group_index * group_rows, group_rows, 1)
        return lax.cond(jnp.any(mask_here), first_live, lambda state: state, carried)

    row_top, total = lax.fori_loop(0, group_total, first_pass, (top_init, total_init))
    log_sum = row_top + jnp.log(total)

    def second_pass(group_index, acc):

        def second_live(acc_in):
            scores, group_kv, group_mask = group_scores(group_index)
            probabilities = jnp.exp(
                jnp.where(group_mask[None], scores - log_sum, far_below)
            ).astype(jnp.bfloat16)
            return acc_in + jnp.einsum(
                "gtk,kd->tgd", probabilities, group_kv[:, AD:], preferred_element_type=jnp.float32
            )

        mask_here = lax.dynamic_slice_in_dim(keep_mask, group_index * group_rows, group_rows, 1)
        return lax.cond(jnp.any(mask_here), second_live, lambda acc_in: acc_in, acc)

    result = lax.fori_loop(
        0, group_total, second_pass, jnp.zeros((tok_rows, q_heads, AD), jnp.float32)
    )
    return (result.astype(jnp.bfloat16), log_sum)


def attend_back(query_rows, window_kv, keep_mask, log_sum, out_rows, grad_rows):
    key_rows = window_kv[:, :AD]
    value_rows = window_kv[:, AD:]
    scores = jnp.einsum(
        "tgd,kd->gtk", query_rows, key_rows, preferred_element_type=jnp.float32
    ) * AD ** (-0.5)
    probabilities = jnp.exp(jnp.where(keep_mask[None], scores - log_sum, far_below))
    row_delta = jnp.sum(grad_rows.astype(jnp.float32) * out_rows.astype(jnp.float32), axis=-1).T
    grad_probs = jnp.einsum(
        "tgd,kd->gtk", grad_rows, value_rows, preferred_element_type=jnp.float32
    )
    grad_scores = (probabilities * (grad_probs - row_delta[:, :, None])).astype(jnp.bfloat16)
    probs_rounded = probabilities.astype(jnp.bfloat16)
    grad_query = jnp.einsum(
        "gtk,kd->tgd", grad_scores, key_rows, preferred_element_type=jnp.float32
    ) * AD ** (-0.5)
    grad_keys = jnp.einsum(
        "gtk,tgd->kd", grad_scores, query_rows, preferred_element_type=jnp.float32
    ) * AD ** (-0.5)
    grad_values = jnp.einsum(
        "gtk,tgd->kd", probs_rounded, grad_rows, preferred_element_type=jnp.float32
    )
    return (grad_query, jnp.concatenate([grad_keys, grad_values], axis=-1))


def column_ends(parts):
    ends = []
    for part in parts[:-1]:
        ends.append(part.shape[1] + (ends[-1] if ends else 0))
    return ends


def times_rows(left, right):
    return jnp.einsum("tc,dc->td", left, right, preferred_element_type=jnp.float32)


def scatter_sum(parts):
    packed = jnp.concatenate([part.astype(jnp.bfloat16) for part in parts], axis=1)
    return lax.psum_scatter(packed, "seq", scatter_dimension=0, tiled=True).astype(jnp.float32)


def product_t(left, right):
    return jnp.einsum("tc,td->cd", left, right, preferred_element_type=jnp.float32)


def local(
    x_in,
    seg_ids,
    decay_exp,
    cotangent,
    w_zx,
    w_bc,
    w_dt,
    w_mout,
    w_q,
    w_kv,
    w_ao,
    w_gu,
    w_down,
    norm1_gain,
    norm2_gain,
    mnorm_gain,
    conv_x,
    conv_bc,
    dt_bias,
    skip_d,
):
    tok_rows = x_in.shape[0]
    seq_count = lax.axis_size("seq")
    reach_blocks = tok_rows * seq_count * 3 // 4 // tok_rows + 1
    window_blocks = (reach_blocks + group_blocks - 1) // group_blocks * group_blocks
    lead_blocks = window_blocks - reach_blocks
    group_total = window_blocks // group_blocks
    group_rows = group_blocks * tok_rows
    tap_count = conv_x.shape[0]
    pad_rows = window_blocks * tok_rows
    seq_index = lax.axis_index("seq")
    start_row = seq_index * tok_rows
    token_ids = jnp.arange(tok_rows, dtype=jnp.int32)
    positions = start_row + token_ids
    seg_front = jnp.concatenate([jnp.full((pad_rows,), -1, jnp.int32), seg_ids])
    own_seg = lax.dynamic_slice_in_dim(seg_front, start_row + pad_rows, tok_rows)
    conv_seg = lax.dynamic_slice_in_dim(
        seg_front, start_row + pad_rows - tap_count + 1, tok_rows + tap_count - 1
    )
    key_seg = lax.dynamic_slice_in_dim(seg_front, start_row + tok_rows, window_blocks * tok_rows)
    prev_seg = conv_seg[tap_count - 2]
    pair_keep = (token_ids[:, None] >= token_ids[None, :]) & (own_seg[:, None] == own_seg[None, :])
    first_keep = (own_seg == prev_seg).astype(jnp.float32)
    last_keep = (own_seg == own_seg[-1]).astype(jnp.float32)
    conv_keeps = conv_masks(conv_seg, tap_count)
    key_pos = (
        start_row
        - (window_blocks - 1) * tok_rows
        + jnp.arange(window_blocks * tok_rows, dtype=jnp.int32)
    )
    attn_keep = (key_pos[None, :] <= positions[:, None]) & (key_seg[None, :] == own_seg[:, None])
    shard_rows, _, inner_half = w_zx.shape
    ff_half = w_gu.shape[2]
    heads_here = w_dt.shape[1]
    width = x_in.shape[1]
    q_width = w_q.shape[1]
    in_parts = (w_zx.reshape(shard_rows, -1), w_bc, w_q, w_kv.reshape(shard_rows, -1), w_dt)
    out_parts = (w_mout.T, w_ao.T)
    ff_parts = (w_gu.reshape(shard_rows, -1), w_down.T)
    in_full, out_full, ff_full = [
        lax.all_gather(jnp.concatenate(parts, axis=1), "seq", axis=0, tiled=True)
        for parts in (in_parts, out_parts, ff_parts)
    ]
    in_ends = column_ends(in_parts)
    mout_full, attn_out_full = jnp.split(out_full, column_ends(out_parts), axis=1)
    gateup_full, down_full = jnp.split(ff_full, column_ends(ff_parts), axis=1)
    x_float = x_in.astype(jnp.float32)
    norm_one = lax.rsqrt(jnp.mean(x_float * x_float, axis=-1, keepdims=True) + epsilon)
    normed = (x_float * norm_one * norm1_gain).astype(jnp.bfloat16)
    zx_proj, bc_proj, q_proj, keyval, dt_proj = jnp.split(
        jnp.dot(normed, in_full, preferred_element_type=jnp.float32), in_ends, axis=1
    )
    gate_z = zx_proj[:, :inner_half]
    x_send = zx_proj[:, inner_half:].astype(jnp.bfloat16)
    bc_send = bc_proj.astype(jnp.bfloat16)
    dt_raw = dt_proj + dt_bias
    edge_x, edge_bc = from_behind(
        (x_send[tok_rows - tap_count + 1 :], bc_send[tok_rows - tap_count + 1 :]), "seq", 1
    )
    ext_x = jnp.concatenate([edge_x, x_send], 0).astype(jnp.float32)
    ext_bc = jnp.concatenate([edge_bc, bc_send], 0).astype(jnp.float32)
    pre_x = conv_apply(ext_x, conv_keeps, conv_x)
    pre_bc = conv_apply(ext_bc, conv_keeps, conv_bc)
    conv_xs = jax.nn.silu(pre_x)
    conv_bcs = jax.nn.silu(pre_bc)
    b_matrix = conv_bcs[:, :NS]
    c_matrix = conv_bcs[:, NS:]
    step_size = jax.nn.softplus(dt_raw)
    rate = -jnp.exp2(-decay_exp.astype(jnp.float32)) * (256.0 / TOK_DEV)
    log_decay = step_size * rate[None, :]
    zero_state = jnp.zeros((heads_here, MP, NS), jnp.float32)
    local_end, local_carry = ssd_end(
        conv_xs, b_matrix, log_decay, step_size, zero_state, first_keep, last_keep
    )
    state_in = entering(local_carry, local_end, False)
    ssd_y = ssd_out(
        conv_xs, b_matrix, c_matrix, log_decay, step_size, state_in, skip_d, pair_keep, first_keep
    )
    silu_z = jax.nn.silu(gate_z)
    gated = ssd_y * silu_z
    square_part = jnp.sum(gated * gated, axis=-1)
    mamba_in = (gated * mnorm_gain).astype(jnp.bfloat16)
    mamba_part = times_rows(mamba_in, mout_full)
    q_heads = q_width // AD
    query_raw = q_proj.reshape(tok_rows, q_heads, AD)
    query16 = rotate(query_raw, positions, 1.0).astype(jnp.bfloat16)
    key_rot = rotate(keyval[:, None, :AD] * key_multiplier, positions, 1.0)[:, 0, :]
    kv_send = jnp.concatenate([key_rot, keyval[:, AD:]], axis=-1).astype(jnp.bfloat16)
    reached = double_window(kv_send, reach_blocks, tok_rows)
    window_flat = jnp.concatenate(
        [jnp.zeros((lead_blocks * tok_rows, 2 * AD), jnp.bfloat16), reached], 0
    )
    attn_out16, log_sum = attend(query16, window_flat, attn_keep, group_rows, group_total)
    attn_flat = attn_out16.reshape(tok_rows, q_heads * AD)
    attn_part = times_rows(attn_flat, attn_out_full)
    square_sum = head_sum(square_part)
    mamba_sum = head_sum(mamba_part)
    attn_sum = head_sum(attn_part)
    mamba_scale = lax.rsqrt(square_sum / MI + epsilon)[:, None]
    hidden_one = (
        x_float + mamba_multiplier * mamba_scale * mamba_sum + attention_multiplier * attn_sum
    )
    norm_two = lax.rsqrt(jnp.mean(hidden_one * hidden_one, axis=-1, keepdims=True) + epsilon)
    normed_two = (hidden_one * norm_two * norm2_gain).astype(jnp.bfloat16)
    gateup = jnp.dot(normed_two, gateup_full, preferred_element_type=jnp.float32)
    gate_pre = gateup[:, :ff_half] * gate_multiplier
    up_proj = gateup[:, ff_half:]
    gate_act = jax.nn.silu(gate_pre)
    ff_hidden = (gate_act * up_proj).astype(jnp.bfloat16)
    ff_part = times_rows(ff_hidden, down_full)
    ff_sum = head_sum(ff_part.astype(jnp.bfloat16))
    output = (hidden_one + down_multiplier * ff_sum).astype(jnp.bfloat16)
    grad_out = cotangent.astype(jnp.float32)
    grad_ff = (down_multiplier * grad_out).astype(jnp.bfloat16)
    grad_hidden = jnp.dot(grad_ff, down_full, preferred_element_type=jnp.float32)
    silu_slope = silu_grad(gate_pre)
    grad_gateup = jnp.concatenate(
        [grad_hidden * up_proj * silu_slope * gate_multiplier, grad_hidden * gate_act], axis=-1
    ).astype(jnp.bfloat16)
    grad_two_part = times_rows(grad_gateup, gateup_full)
    grad_normed_two = head_sum(grad_two_part)
    ff_shard = scatter_sum((product_t(normed_two, grad_gateup), product_t(grad_ff, ff_hidden)))
    shard_gu = ff_shard[:, : 2 * ff_half].reshape(shard_rows, 2, ff_half)
    shard_down = ff_shard[:, 2 * ff_half :].T
    scaled_two = grad_normed_two * norm2_gain
    grad_gain_two = jnp.sum(grad_normed_two * hidden_one * norm_two, axis=0)
    grad_hidden_one = (
        grad_out
        + norm_two * scaled_two
        - hidden_one * norm_two**3 * jnp.mean(scaled_two * hidden_one, axis=-1, keepdims=True)
    )
    grad_mamba16 = (mamba_multiplier * mamba_scale * grad_hidden_one).astype(jnp.bfloat16)
    grad_scale = mamba_multiplier * jnp.sum(grad_hidden_one * mamba_sum, axis=-1, keepdims=True)
    grad_attn16 = (attention_multiplier * grad_hidden_one).astype(jnp.bfloat16)
    out_shard = scatter_sum((product_t(grad_mamba16, mamba_in), product_t(grad_attn16, attn_flat)))
    shard_mout = out_shard[:, :inner_half].T
    shard_ao = out_shard[:, inner_half:].T
    grad_mamba_in = jnp.dot(grad_mamba16, mout_full, preferred_element_type=jnp.float32)
    grad_mnorm = jnp.sum(grad_mamba_in * gated, axis=0)
    grad_gated = mnorm_gain * grad_mamba_in - grad_scale * mamba_scale**3 * gated / MI
    grad_ssd_y = grad_gated * silu_z
    grad_z = grad_gated * ssd_y * silu_grad(gate_z)

    def out_part(chan_in, b_in, c_in, log_in, step_in, state_given, skip_in):
        return ssd_out(
            chan_in, b_in, c_in, log_in, step_in, state_given, skip_in, pair_keep, first_keep
        )

    _, pull_out = jax.vjp(
        out_part, conv_xs, b_matrix, c_matrix, log_decay, step_size, state_in, skip_d
    )
    (
        grad_xs_one,
        grad_b_one,
        grad_c_one,
        grad_log_one,
        grad_step_one,
        grad_state_local,
        grad_skip,
    ) = pull_out(grad_ssd_y)
    grad_state_end = entering(local_carry, grad_state_local, True)

    def end_part(chan_in, b_in, log_in, step_in):
        return ssd_end(chan_in, b_in, log_in, step_in, state_in, first_keep, last_keep)[0]

    _, pull_end = jax.vjp(end_part, conv_xs, b_matrix, log_decay, step_size)
    grad_xs_two, grad_b_two, grad_log_two, grad_step_two = pull_end(grad_state_end)
    grad_step = grad_step_one + grad_step_two + (grad_log_one + grad_log_two) * rate[None, :]
    grad_dt_raw = grad_step * jax.nn.sigmoid(dt_raw)
    grad_dt_bias = jnp.sum(grad_dt_raw, axis=0)
    grad_pre_x = (grad_xs_one + grad_xs_two) * silu_grad(pre_x)
    grad_pre_bc = jnp.concatenate([grad_b_one + grad_b_two, grad_c_one], axis=-1) * silu_grad(
        pre_bc
    )
    grad_ext_x, grad_conv_x = conv_grads(ext_x, conv_keeps, conv_x, grad_pre_x)
    grad_ext_bc, grad_conv_bc = conv_grads(ext_bc, conv_keeps, conv_bc, grad_pre_bc)
    back_x, back_bc = from_behind(
        (grad_ext_x[: tap_count - 1], grad_ext_bc[: tap_count - 1]), "seq", -1
    )
    grad_x_send = grad_ext_x[tap_count - 1 :].at[tok_rows - tap_count + 1 :].add(back_x)
    grad_bc_send = grad_ext_bc[tap_count - 1 :].at[tok_rows - tap_count + 1 :].add(back_bc)
    grad_zx16 = jnp.concatenate([grad_z, grad_x_send], axis=-1).astype(jnp.bfloat16)
    grad_bc16 = grad_bc_send.astype(jnp.bfloat16)
    grad_dt16 = grad_dt_raw.astype(jnp.bfloat16)
    grad_heads16 = (
        jnp.dot(grad_attn16, attn_out_full, preferred_element_type=jnp.float32)
        .astype(jnp.bfloat16)
        .reshape(tok_rows, q_heads, AD)
    )

    def back_group(group_index, carried):
        query_acc, window_grads = carried
        start = group_index * group_rows
        group_kv = lax.dynamic_slice_in_dim(window_flat, start, group_rows)
        group_mask = lax.dynamic_slice_in_dim(attn_keep, start, group_rows, 1)

        def back_live(unused):
            return attend_back(query16, group_kv, group_mask, log_sum, attn_out16, grad_heads16)

        def dead(unused):
            return (
                jnp.zeros((tok_rows, q_heads, AD), jnp.float32),
                jnp.zeros((group_rows, 2 * AD), jnp.float32),
            )

        part_query, part_window = lax.cond(jnp.any(group_mask), back_live, dead, 0)
        return (
            query_acc + part_query,
            lax.dynamic_update_slice_in_dim(window_grads, part_window, start, 0),
        )

    grad_query, grad_window = lax.fori_loop(
        0,
        group_total,
        back_group,
        (
            jnp.zeros((tok_rows, q_heads, AD), jnp.float32),
            jnp.zeros((window_blocks * tok_rows, 2 * AD), jnp.float32),
        ),
    )
    grad_kv_own = double_back(grad_window[lead_blocks * tok_rows :], reach_blocks, tok_rows)
    grad_q16 = (
        rotate(grad_query, positions, -1.0).reshape(tok_rows, q_heads * AD).astype(jnp.bfloat16)
    )
    grad_key = rotate(grad_kv_own[:, None, :AD], positions, -1.0)[:, 0, :] * key_multiplier
    grad_kv16 = jnp.concatenate([grad_key, grad_kv_own[:, AD:]], axis=-1).astype(jnp.bfloat16)
    grad_in16 = jnp.concatenate([grad_zx16, grad_bc16, grad_q16, grad_kv16, grad_dt16], axis=1)
    in_shard = scatter_sum((product_t(normed, grad_in16),))
    shard_zx, shard_bc_part, shard_q, shard_kv, shard_dt = jnp.split(in_shard, in_ends, axis=1)
    shard_zx = shard_zx.reshape(shard_rows, 2, inner_half)
    shard_kv = shard_kv.reshape(shard_rows, 2, -1)
    shard_bc = head_sum(shard_bc_part)
    grad_normed_sum = head_sum(times_rows(grad_in16, in_full).astype(jnp.bfloat16))
    scaled_one = grad_normed_sum * norm1_gain
    grad_gain_one = jnp.sum(grad_normed_sum * x_float * norm_one, axis=0)
    x_grad = (
        grad_hidden_one
        + norm_one * scaled_one
        - x_float * norm_one**3 * jnp.mean(scaled_one * x_float, axis=-1, keepdims=True)
    )
    small_parts = (
        grad_gain_one,
        grad_gain_two,
        grad_mnorm,
        grad_conv_x,
        grad_conv_bc,
        grad_dt_bias,
        grad_skip,
    )
    small_sum = seq_sum(jnp.concatenate([part.reshape(-1) for part in small_parts]))
    small_out = []
    start = 0
    for part in small_parts:
        small_out.append(small_sum[start : start + part.size].reshape(part.shape))
        start = start + part.size
    sum_gain_one, sum_gain_two, sum_mnorm, sum_conv_x, conv_bc_part, sum_dt_bias, sum_skip = (
        small_out
    )
    sum_conv_bc = head_sum(conv_bc_part)
    return (
        output,
        x_grad,
        shard_zx,
        shard_bc,
        shard_dt,
        shard_mout,
        shard_q,
        shard_kv,
        shard_ao,
        shard_gu,
        shard_down,
        sum_gain_one,
        sum_gain_two,
        sum_mnorm,
        sum_conv_x,
        sum_conv_bc,
        sum_dt_bias,
        sum_skip,
    )


def solution(mesh):
    in_specs = (
        P("seq", None),
        P(),
        P("head"),
        P("seq", None),
        P("seq", None, "head"),
        P("seq", None),
        P("seq", "head"),
        P("head", "seq"),
        P("seq", "head"),
        P("seq", None, "head"),
        P("head", "seq"),
        P("seq", None, "head"),
        P("head", "seq"),
        P(),
        P(),
        P("head"),
        P(None, "head"),
        P(),
        P("head"),
        P("head"),
    )
    out_specs = (
        P("seq", None),
        P("seq", None),
        P("seq", None, "head"),
        P("seq", None),
        P("seq", "head"),
        P("head", "seq"),
        P("seq", "head"),
        P("seq", None, "head"),
        P("head", "seq"),
        P("seq", None, "head"),
        P("head", "seq"),
        P(),
        P(),
        P("head"),
        P(None, "head"),
        P(),
        P("head"),
        P("head"),
    )
    return jax.shard_map(local, mesh=mesh, in_specs=in_specs, out_specs=out_specs, check_vma=False)
```
